32 devices in a mesh: col: 4 (over z), row: 8 (over y, x, core).
Axes of the slice: x: 2, y: 2, z: 4, core: 2. Of those that a mesh axis runs over, the one named last changes fastest.
Arguments:
- matrix: float32 [8192, 8192], P('row', 'col'), may hold values from -6 to 6
- pattern: int32 [32, 4], P('row'), may hold values 0 or 1
- active: int32 [8, 4, 24, 2], P('row', 'col'), may hold values from 0 to 7, as said below
- pivots: int32 [4], replicated, may hold values from 0 to 31, as said below
- lower_inv: float32 [4, 256, 256], replicated, may hold values from -0.3 to 0.3, as said below
- upper_inv: float32 [4, 256, 256], replicated, may hold values from -0.3 to 0.3, as said below
Outputs:
- factored: float32 [8192, 8192], P('row', 'col')
The draws below stay inside these ranges and needn't reach their ends.
Inputs may be any that keep to these rules, and one draw needn't show every extreme that they name: For each device (a, b), active[a, b] holds 24 distinct pairs (l, c) with l below 4 and c below 8. `pivots`: 4 distinct block rows of the window, among them always the first and the last block row. `lower_inv`: each block is lower triangular with a positive diagonal. `upper_inv`: each block is upper triangular with a positive diagonal.
All inputs are finite; a program needn't handle non-finite values. No bound on the sum of `pattern` on one device may be relied on, other than what follows from the above.
Results may differ from the reference program's by a relative error of at most 0.0001.
Values sent between devices are 32-bit elements; how exact they have to be, the bound alone decides.
A program may use at most 128 MiB of HBM per device.

```python
import jax
import jax.numpy as jnp
from jax import lax

BLOCK_SIZE = 256
PANELS = 4
RL = 4
CL = 8
ACT = 24
PR = 8
PC = 4
NR = 32
NC = 32


def draw_active(key, part):
    device_keys = jax.random.split(jax.random.fold_in(key, 3), PR * PC)

    def one_device(sub_key):
        chosen = jax.random.permutation(sub_key, RL * CL)[:ACT]
        return jnp.stack([chosen // CL, chosen % CL], axis=1).astype(jnp.int32)
    return jax.vmap(one_device)(device_keys).reshape(PR, PC, ACT, 2)


def draw_pivots(key, part):
    middle = jax.random.permutation(jax.random.fold_in(key, 5), NR - 2)[:PANELS - 2].astype(jnp.int32) + 1
    ends = jnp.array([0, NR - 1], dtype=jnp.int32)
    chosen = jnp.concatenate([ends, middle])
    order = jax.random.permutation(jax.random.fold_in(key, 6), PANELS)
    return chosen[order].astype(jnp.int32)


def inverse_blocks(key, lower_side):
    noise_key = jax.random.fold_in(key, 11)
    gain_key = jax.random.fold_in(key, 12)
    noise = jax.random.normal(noise_key, (PANELS, BLOCK_SIZE, BLOCK_SIZE), jnp.float32)
    noise = jnp.clip(noise, -4.0, 4.0) * (0.6 / BLOCK_SIZE ** 0.5)
    if lower_side:
        noise = jnp.tril(noise, -1)
    else:
        noise = jnp.triu(noise, 1)
    gains = jax.random.uniform(gain_key, (PANELS, 1, BLOCK_SIZE), jnp.float32, 0.6, 1.4)
    return 0.2 * (jnp.eye(BLOCK_SIZE, dtype=jnp.float32)[None] * gains + noise)


def draw_lower_inv(key, part):
    return inverse_blocks(jax.random.fold_in(key, 21), True)


def draw_upper_inv(key, part):
    return inverse_blocks(jax.random.fold_in(key, 22), False)


def touch_ends(drawn, key, smallest, largest):
    longest = drawn.shape.index(max(drawn.shape))
    spots = []
    for shift in (0, 1):
        where = [jax.random.randint(jax.random.fold_in(key, axis), (), 0, length) for axis, length in enumerate(drawn.shape)]
        where[longest] = (where[longest] + shift) % drawn.shape[longest]
        spots.append(tuple(where))
    return drawn.at[spots[0]].set(smallest).at[spots[1]].set(largest)


def level_of(rng, dims, pieces, low, largest):
    factor_of = 1.0
    for position, parts in pieces:
        draws = jax.random.uniform(jax.random.fold_in(jax.random.fold_in(rng, 6), position), (parts,), jnp.float32, low / len(pieces), largest / len(pieces))
        factor_of = factor_of * jnp.repeat(jnp.exp(draws), dims[position] // parts).reshape((-1,) + (1,) * (len(dims) - 1 - position))
    return factor_of


def centred(rng, extent, scale, bound, cuts=(), held_as=jnp.bfloat16):
    entries = jax.random.normal(rng, extent, jnp.float32) * scale
    if len(cuts) > 0:
        entries = level_of(rng, extent, cuts, -0.22, 0.18) * entries
    return jnp.clip(entries, min=-bound, max=bound).astype(held_as)


def setup_inputs(seed: int = 0) -> dict:
    arg_keys = jax.random.split(jax.random.key(seed), 7)
    return {
        "matrix": centred(arg_keys[0], (NR * BLOCK_SIZE, NC * BLOCK_SIZE), 1.0, 6.0, ((0, 8), (1, 4)), jnp.float32),
        "pattern": touch_ends((jax.random.randint(arg_keys[1], (NR, PANELS), 0, 4) < 3).astype(jnp.int32), jax.random.fold_in(arg_keys[1], 1), 0, 1),
        "active": draw_active(jax.random.fold_in(arg_keys[6], 71), 0),
        "pivots": draw_pivots(jax.random.fold_in(arg_keys[6], 71), 0),
        "lower_inv": draw_lower_inv(jax.random.fold_in(arg_keys[6], 71), 0),
        "upper_inv": draw_upper_inv(jax.random.fold_in(arg_keys[6], 71), 0),
    }


def reference(matrix, pattern, active, pivots, lower_inv, upper_inv):
    highest = lax.Precision.HIGHEST
    dev_rows = jnp.arange(PR, dtype=jnp.int32)[:, None, None]
    dev_cols = jnp.arange(PC, dtype=jnp.int32)[None, :, None]
    live_rows = (dev_rows * RL + active[:, :, :, 0]).reshape(-1).astype(jnp.int32)
    live_cols = (dev_cols * CL + active[:, :, :, 1]).reshape(-1).astype(jnp.int32)
    remaining_tiles = jnp.zeros((NR, NC), jnp.int32).at[live_rows, live_cols].set(1)
    block_row_count = jnp.arange(NR, dtype=jnp.int32)
    block_cols = jnp.arange(NC, dtype=jnp.int32)
    factored = matrix
    for present_panel in range(PANELS):
        elimination_rows = jnp.any(block_row_count[:, None] == pivots[None, :present_panel + 1], axis=1)
        finished_columns = (block_cols % CL == 0) & (block_cols // CL <= present_panel)
        column = present_panel * CL
        raw_col = factored[:, column * BLOCK_SIZE:(column + 1) * BLOCK_SIZE]
        keep_mask = jnp.repeat((pattern[:, present_panel] != 0).astype(jnp.float32), BLOCK_SIZE)[:, None]
        lower_tile_grid = jnp.dot(raw_col, upper_inv[present_panel], precision=highest, preferred_element_type=jnp.float32) * keep_mask
        pivot_row = pivots[present_panel].astype(jnp.int32)
        raw_row = lax.dynamic_slice_in_dim(factored, pivot_row * BLOCK_SIZE, BLOCK_SIZE, 0)
        upper_tiles = jnp.dot(lower_inv[present_panel], raw_row, precision=highest, preferred_element_type=jnp.float32)
        permitted_entries = (remaining_tiles != 0) & jnp.logical_not(elimination_rows)[:, None] & jnp.logical_not(finished_columns)[None, :]

        def update_row(row_item):
            row_block, low_tile, row_ok = row_item
            product = jnp.dot(low_tile, upper_tiles, precision=highest, preferred_element_type=jnp.float32)
            return row_block - jnp.where(jnp.repeat(row_ok, BLOCK_SIZE)[None, :], product, 0.0)

        updated = lax.map(update_row, (factored.reshape(NR, BLOCK_SIZE, NC * BLOCK_SIZE), lower_tile_grid.reshape(NR, BLOCK_SIZE, BLOCK_SIZE), permitted_entries))
        factored = updated.reshape(NR * BLOCK_SIZE, NC * BLOCK_SIZE)
        column_present = factored[:, column * BLOCK_SIZE:(column + 1) * BLOCK_SIZE]
        fresh_column = jnp.where(jnp.repeat(jnp.logical_not(elimination_rows), BLOCK_SIZE)[:, None], lower_tile_grid, column_present)
        factored = factored.at[:, column * BLOCK_SIZE:(column + 1) * BLOCK_SIZE].set(fresh_column)
        row_now = lax.dynamic_slice_in_dim(factored, pivot_row * BLOCK_SIZE, BLOCK_SIZE, 0)
        new_row = jnp.where(jnp.repeat(jnp.logical_not(finished_columns), BLOCK_SIZE)[None, :], upper_tiles, row_now)
        factored = lax.dynamic_update_slice_in_dim(factored, new_row, pivot_row * BLOCK_SIZE, 0)
    return factored
```

```python
import functools

import jax
import jax.numpy as jnp
from jax import lax
from jax.experimental import pallas as pl
from jax.experimental.pallas import tpu as pltpu
from jax.sharding import PartitionSpec as P

CHUNKS = 8


def mm(left, right):
    return jnp.dot(
        left, right, precision=lax.Precision.HIGHEST, preferred_element_type=jnp.float32
    )


def bcast_kernel(root, row_size, axes, src, out, ring_send, ring_recv, sib_send, sib_recv, own_sem):
    chips = row_size // 2
    side = max(chips // 2, 1)
    half = src.shape[0] // 2
    step = half // CHUNKS
    me = lax.axis_index("row")
    chip, core = me // 2, me % 2
    y, x = chip // 2, chip % 2
    pos = y + x * (2 * side - 1 - 2 * y)
    root_chip, root_core = root // 2, root % 2
    root_pos = root_chip // 2 + (root_chip % 2) * (2 * side - 1 - 2 * (root_chip // 2))
    sign = 1 - 2 * core
    rel = ((pos - root_pos) * sign + chips) % chips
    nxt_pos = (pos + sign + chips) % chips
    nx = nxt_pos // side
    ny = nxt_pos + nx * (2 * side - 1 - 2 * nxt_pos)
    nxt_row = (ny * 2 + nx) * 2 + core
    sib_row = chip * 2 + 1 - core

    def device(row):
        return tuple(row if name == "row" else lax.axis_index(name) for name in axes)

    def rows(part, index):
        return pl.ds(pl.multiple_of(part * half + index * step, 8), step)

    def ring(ref, index):
        return pltpu.make_async_remote_copy(
            src_ref=ref.at[rows(core, index)],
            dst_ref=out.at[rows(core, index)],
            send_sem=ring_send.at[index],
            recv_sem=ring_recv.at[index],
            device_id=device(nxt_row),
            device_id_type=pl.DeviceIdType.MESH,
        )

    def sib(ref, kind, part, index):
        return pltpu.make_async_remote_copy(
            src_ref=ref.at[rows(part, index)],
            dst_ref=out.at[rows(part, index)],
            send_sem=sib_send.at[kind, index],
            recv_sem=sib_recv.at[kind, index],
            device_id=device(sib_row),
            device_id_type=pl.DeviceIdType.MESH,
        )

    def loop(fn):
        def one(index, carry):
            fn(index)
            return carry

        lax.fori_loop(0, CHUNKS, one, 0)

    @pl.when(me == root)
    def _():
        def go(index):
            sib(src, 0, 1 - core, index).start()
            ring(src, index).start()

        loop(go)
        loop(lambda index: sib(src, 1, core, index).start())
        own = pltpu.make_async_copy(src, out, own_sem)
        own.start()
        own.wait()

        def done(index):
            sib(src, 0, 1 - core, index).wait_send()
            sib(src, 1, core, index).wait_send()
            ring(src, index).wait_send()

        loop(done)

    @pl.when((rel == 0) & (me != root))
    def _():
        def go(index):
            sib(out, 0, core, index).wait_recv()
            ring(out, index).start()

        loop(go)

        def done(index):
            sib(out, 1, 1 - core, index).wait_recv()
            ring(out, index).wait_send()

        loop(done)

    @pl.when(rel != 0)
    def _():
        def go(index):
            ring(out, index).wait_recv()

            @pl.when(rel != chips - 1)
            def _():
                ring(out, index).start()

            sib(out, 1, core, index).start()

        loop(go)

        def done(index):
            sib(out, 1, 1 - core, index).wait_recv()
            sib(out, 1, core, index).wait_send()

            @pl.when(rel != chips - 1)
            def _():
                ring(out, index).wait_send()

        loop(done)


def bcast(block, owner, row_size, axes):
    def branch(root):
        return pl.pallas_call(
            functools.partial(bcast_kernel, root, row_size, axes),
            out_shape=jax.ShapeDtypeStruct(block.shape, block.dtype),
            in_specs=[pl.BlockSpec(memory_space=pl.ANY)],
            out_specs=pl.BlockSpec(memory_space=pl.ANY),
            scratch_shapes=[
                pltpu.SemaphoreType.DMA((CHUNKS,)),
                pltpu.SemaphoreType.DMA((CHUNKS,)),
                pltpu.SemaphoreType.DMA((2, CHUNKS)),
                pltpu.SemaphoreType.DMA((2, CHUNKS)),
                pltpu.SemaphoreType.DMA,
            ],
            compiler_params=pltpu.CompilerParams(has_side_effects=True),
            name=f"bcast_{root}_{block.shape[1]}",
        )

    return lax.switch(owner, [branch(root) for root in range(row_size)], block)


def body(mesh, matrix, pattern, active, pivots, lower_inv, upper_inv):
    tile = lower_inv.shape[1]
    panels = lower_inv.shape[0]
    height, width = matrix.shape
    rows_loc, cols_loc = height // tile, width // tile
    row_size, col_size = mesh.shape["row"], mesh.shape["col"]
    axes = tuple(mesh.axis_names)
    row_dev = lax.axis_index("row")
    holder = lax.axis_index("col")
    local_rows = jnp.arange(rows_loc, dtype=jnp.int32)
    local_cols = jnp.arange(cols_loc, dtype=jnp.int32)
    global_rows = row_dev * rows_loc + local_rows
    owner = pivots // rows_loc
    owner_loc = pivots % rows_loc

    live_local = jnp.zeros((rows_loc, cols_loc), jnp.float32).at[
        active[0, 0, :, 0], active[0, 0, :, 1]
    ].set(1.0)
    flags = jnp.concatenate([live_local.reshape(-1), pattern.astype(jnp.float32).reshape(-1)])
    flags = lax.all_gather(flags, ("row", "col"), axis=0, tiled=False)
    flags = flags.reshape(row_size, col_size, -1)
    cells = rows_loc * cols_loc
    live = flags[:, :, :cells].reshape(row_size, col_size, rows_loc, cols_loc)
    live = live.transpose(0, 2, 1, 3).reshape(row_size * rows_loc, col_size, cols_loc)
    pattern_all = flags[:, 0, cells:].reshape(row_size * rows_loc, panels)
    live_mine = lax.dynamic_slice_in_dim(live, row_dev * rows_loc, rows_loc, 0)
    col_flag = live_mine[:, :panels, 0]
    row_flag = lax.dynamic_index_in_dim(live, holder, 1, keepdims=False)[pivots]
    cross_flag = live[pivots][:, :panels, 0]
    pivot_pattern = pattern_all[pivots]

    strips = lax.all_gather(matrix[:, :tile], "col", axis=0, tiled=False)

    def send_row(carry, item):
        who, where = item
        block = lax.dynamic_slice(matrix, (where * tile, 0), (tile, width))
        return carry, bcast(block, who, row_size, axes)

    _, row_raw = lax.scan(send_row, 0, (owner, owner_loc))

    def send_cross(carry, item):
        who, where = item
        block = lax.dynamic_slice(strips, (0, where * tile, 0), (panels, tile, tile))
        block = block.transpose(1, 0, 2).reshape(tile, panels * tile)
        return carry, bcast(block, who, row_size, axes)

    _, cross_raw = lax.scan(send_cross, 0, (owner, owner_loc))

    def tall(mask):
        return jnp.repeat(mask.astype(jnp.float32), tile)[:, None]

    def wide(mask):
        return jnp.repeat(mask.astype(jnp.float32), tile)[None, :]

    cross = cross_raw.reshape(panels * tile, panels * tile)
    cols = jnp.concatenate([strips[k] for k in range(panels)], axis=1)
    rows = row_raw.reshape(panels * tile, width)
    lowers, uppers = [], []
    for k in range(panels):
        gone = jnp.any(global_rows[:, None] == pivots[None, : k + 1], axis=1)
        opened = jnp.logical_not((local_cols == 0) & (holder <= k))
        lower = mm(cols[:, :tile], upper_inv[k]) * tall(pattern[:, k] != 0)
        upper = mm(lower_inv[k], rows[:tile])
        lowers.append(lower)
        uppers.append(upper)
        if k + 1 < panels:
            low_x = mm(cross[tile:, :tile], upper_inv[k]) * tall(pivot_pattern[k + 1 :, k])
            up_x = mm(lower_inv[k], cross[:tile, tile:])
            ok = jnp.repeat(jnp.repeat(cross_flag[k + 1 :, k + 1 :], tile, 0), tile, 1)
            cross = cross[tile:, tile:] - jnp.where(ok != 0, mm(low_x, up_x), 0.0)
            col_ok = (col_flag[:, k + 1 :] != 0) & jnp.logical_not(gone)[:, None]
            col_ok = jnp.repeat(jnp.repeat(col_ok, tile, 0), tile, 1)
            col_new = cols[:, tile:] - jnp.where(col_ok, mm(lower, up_x), 0.0)
            here = tall(global_rows == pivots[k]) != 0
            cols = jnp.where(here, jnp.tile(up_x, (rows_loc, 1)), col_new)
            row_ok = (row_flag[k + 1 :] != 0) & opened[None, :]
            row_ok = jnp.repeat(jnp.repeat(row_ok, tile, 0), tile, 1)
            row_new = rows[tile:] - jnp.where(row_ok, mm(low_x, upper), 0.0)
            first = jnp.where(holder == k, low_x, row_new[:, :tile])
            rows = lax.dynamic_update_slice(row_new, first, (0, 0))
    gone = [jnp.any(global_rows[:, None] == pivots[None, : k + 1], axis=1) for k in range(panels)]
    opened = [jnp.logical_not((local_cols == 0) & (holder <= k)) for k in range(panels)]
    left = jnp.concatenate(
        [jnp.where(tall(gone[k]) != 0, 0.0, lowers[k]) for k in range(panels)], axis=1
    )
    right = jnp.concatenate(
        [jnp.where(wide(opened[k]) != 0, uppers[k], 0.0) for k in range(panels)], axis=0
    )
    alive = jnp.repeat(jnp.repeat(live_local != 0, tile, 0), tile, 1)
    out = matrix - jnp.where(alive, mm(left, right), 0.0)
    first = out[:, :tile]
    for k in range(panels):
        first = jnp.where((holder == k) & (tall(gone[k]) == 0), lowers[k], first)
    out = lax.dynamic_update_slice(out, first, (0, 0))
    for k in range(panels):
        at = (owner_loc[k] * tile, jnp.int32(0))
        old = lax.dynamic_slice(out, at, (tile, width))
        new = jnp.where((row_dev == owner[k]) & (wide(opened[k]) != 0), uppers[k], old)
        out = lax.dynamic_update_slice(out, new, at)
    return out


def solution(mesh):
    in_specs = (P("row", "col"), P("row", None), P("row", "col", None, None), P(), P(), P())
    return jax.shard_map(
        functools.partial(body, mesh),
        mesh=mesh,
        in_specs=in_specs,
        out_specs=P("row", "col"),
        check_vma=False,
    )
```

```python
import functools

import jax
import jax.numpy as jnp
from jax import lax
from jax.experimental import pallas as pl
from jax.experimental.pallas import tpu as pltpu
from jax.sharding import PartitionSpec as P

CHUNKS = 8


def mm(left, right):
    return jnp.dot(
        left, right, precision=lax.Precision.HIGHEST, preferred_element_type=jnp.float32
    )


def bcast_kernel(roots, offsets, row_size, axes, src, out, ring_send, ring_recv, sib_send, sib_recv, own_sem):
    chips = row_size // 2
    side = max(chips // 2, 1)
    size = out.shape[0] // len(roots)
    half = size // 2
    step = half // CHUNKS
    me = lax.axis_index("row")
    chip, core = me // 2, me % 2
    y, x = chip // 2, chip % 2
    pos = y + x * (2 * side - 1 - 2 * y)
    sign = 1 - 2 * core
    nxt_pos = (pos + sign + chips) % chips
    nx = nxt_pos // side
    ny = nxt_pos + nx * (2 * side - 1 - 2 * nxt_pos)
    nxt_row = (ny * 2 + nx) * 2 + core
    sib_row = chip * 2 + 1 - core
    count = len(roots)

    def position(root):
        root_chip = root // 2
        return root_chip // 2 + (root_chip % 2) * (2 * side - 1 - 2 * (root_chip // 2))

    rel = [((pos - position(root)) * sign + chips) % chips for root in roots]

    def device(row):
        return tuple(row if name == "row" else lax.axis_index(name) for name in axes)

    def rows(base, part, index):
        return pl.ds(pl.multiple_of(base + part * half + index * step, 8), step)

    def source(b, held, part, index):
        if held:
            return out.at[rows(b * size, part, index)]
        return src.at[rows(offsets[b], part, index)]

    def ring(b, held, index):
        return pltpu.make_async_remote_copy(
            src_ref=source(b, held, core, index),
            dst_ref=out.at[rows(b * size, core, index)],
            send_sem=ring_send.at[b, index],
            recv_sem=ring_recv.at[b, index],
            device_id=device(nxt_row),
            device_id_type=pl.DeviceIdType.MESH,
        )

    def sib(b, held, kind, part, index):
        return pltpu.make_async_remote_copy(
            src_ref=source(b, held, part, index),
            dst_ref=out.at[rows(b * size, part, index)],
            send_sem=sib_send.at[b, kind, index],
            recv_sem=sib_recv.at[b, kind, index],
            device_id=device(sib_row),
            device_id_type=pl.DeviceIdType.MESH,
        )

    def own(b):
        return pltpu.make_async_copy(
            src.at[pl.ds(offsets[b], size)], out.at[pl.ds(b * size, size)], own_sem.at[b]
        )

    def loop(fn):
        def one(index, carry):
            fn(index)
            return carry

        lax.fori_loop(0, CHUNKS, one, 0)

    for b in range(count):

        @pl.when(me == roots[b])
        def _():
            def go(index):
                sib(b, False, 0, 1 - core, index).start()
                ring(b, False, index).start()

            loop(go)
            loop(lambda index: sib(b, False, 1, core, index).start())
            own(b).start()

    def forward(index):
        for b in range(count):

            @pl.when((rel[b] == 0) & (me != roots[b]))
            def _():
                sib(b, True, 0, core, index).wait_recv()
                ring(b, True, index).start()

            @pl.when(rel[b] != 0)
            def _():
                ring(b, True, index).wait_recv()

                @pl.when(rel[b] != chips - 1)
                def _():
                    ring(b, True, index).start()

                sib(b, True, 1, core, index).start()

    loop(forward)

    def done(index):
        for b in range(count):

            @pl.when(me == roots[b])
            def _():
                sib(b, False, 0, 1 - core, index).wait_send()
                sib(b, False, 1, core, index).wait_send()

            @pl.when(me != roots[b])
            def _():
                sib(b, True, 1, 1 - core, index).wait_recv()

            @pl.when(rel[b] != 0)
            def _():
                sib(b, True, 1, core, index).wait_send()

            @pl.when(rel[b] != chips - 1)
            def _():
                ring(b, True, index).wait_send()

    loop(done)
    for b in range(count):

        @pl.when(me == roots[b])
        def _():
            own(b).wait()


def bcast_call(roots, offsets, size, row_size, axes, source):
    count = len(roots)
    return pl.pallas_call(
        functools.partial(bcast_kernel, roots, offsets, row_size, axes),
        out_shape=jax.ShapeDtypeStruct((count * size, source.shape[1]), source.dtype),
        in_specs=[pl.BlockSpec(memory_space=pl.ANY)],
        out_specs=pl.BlockSpec(memory_space=pl.ANY),
        scratch_shapes=[
            pltpu.SemaphoreType.DMA((count, CHUNKS)),
            pltpu.SemaphoreType.DMA((count, CHUNKS)),
            pltpu.SemaphoreType.DMA((count, 2, CHUNKS)),
            pltpu.SemaphoreType.DMA((count, 2, CHUNKS)),
            pltpu.SemaphoreType.DMA((count,)),
        ],
        compiler_params=pltpu.CompilerParams(has_side_effects=True),
        name="_".join(["bcast"] + [str(root) for root in roots] + [str(source.shape[1])]),
    )(source)


def bcast(block, owner, row_size, axes):
    def branch(root):
        return lambda source: bcast_call((root,), (0,), block.shape[0], row_size, axes, source)

    return lax.switch(owner, [branch(root) for root in range(row_size)], block)


def body(mesh, matrix, pattern, active, pivots, lower_inv, upper_inv):
    tile = lower_inv.shape[1]
    panels = lower_inv.shape[0]
    height, width = matrix.shape
    rows_loc, cols_loc = height // tile, width // tile
    row_size = mesh.shape["row"]
    axes = tuple(mesh.axis_names)
    row_dev = lax.axis_index("row")
    holder = lax.axis_index("col")
    local_rows = jnp.arange(rows_loc, dtype=jnp.int32)
    local_cols = jnp.arange(cols_loc, dtype=jnp.int32)
    global_rows = row_dev * rows_loc + local_rows
    owner = pivots // rows_loc
    owner_loc = pivots % rows_loc

    live_local = jnp.zeros((rows_loc, cols_loc), jnp.float32).at[
        active[0, 0, :, 0], active[0, 0, :, 1]
    ].set(1.0)
    pad = jnp.zeros((8, tile), jnp.float32).at[0, :rows_loc].set(live_local[:, 0])

    strips = lax.all_gather(
        jnp.concatenate([matrix[:, :tile], pad], axis=0), "col", axis=0, tiled=False
    )
    strips, strip_flag = strips[:panels, :height], strips[:panels, height, :rows_loc]
    col_flag = strip_flag.T

    rank = jnp.sum(pivots[None, :] < pivots[:, None], axis=1)
    by_row = jnp.sum(
        jnp.where(rank[None, :] == jnp.arange(panels)[:, None], pivots[None, :], 0), axis=1
    )
    middle = (by_row[1:-1] // rows_loc, by_row[1:-1] % rows_loc)
    ends = (0, row_size - 1)

    def gather(ends_got, middle_got):
        size = ends_got.shape[0] // 2
        parts = jnp.concatenate([ends_got[None, :size], middle_got, ends_got[None, size:]], axis=0)
        return [lax.dynamic_index_in_dim(parts, rank[k], 0, keepdims=False) for k in range(panels)]

    def send_row(carry, item):
        who, where = item
        block = lax.dynamic_slice(matrix, (where * tile, 0), (tile, width))
        return carry, bcast(block, who, row_size, axes)

    _, middle_rows = lax.scan(send_row, 0, middle)
    ends_rows = bcast_call(ends, (0, height - tile), tile, row_size, axes, matrix)
    rows = jnp.concatenate(gather(ends_rows, middle_rows), axis=0)

    def crossing(where):
        block = lax.dynamic_slice(strips, (0, where * tile, 0), (panels, tile, tile))
        block = block.transpose(1, 0, 2).reshape(tile, panels * tile)
        words = jnp.concatenate(
            [live_local[where], pattern[where].astype(jnp.float32), strip_flag[:, where]]
        )
        more = jnp.zeros((tile, 128), jnp.float32).at[0, : words.shape[0]].set(words)
        return jnp.concatenate([block, more], axis=1)

    def send_cross(carry, item):
        who, where = item
        return carry, bcast(crossing(where), who, row_size, axes)

    _, middle_cross = lax.scan(send_cross, 0, middle)
    both = jnp.concatenate([crossing(0), crossing(rows_loc - 1)], axis=0)
    ends_cross = bcast_call(ends, (0, tile), tile, row_size, axes, both)
    got = gather(ends_cross, middle_cross)
    cross = jnp.concatenate([part[:, : panels * tile] for part in got], axis=0)
    words = jnp.stack([part[0, panels * tile :] for part in got])
    row_flag = words[:, :cols_loc]
    pivot_pattern = words[:, cols_loc : cols_loc + panels]
    cross_flag = words[:, cols_loc + panels : cols_loc + 2 * panels]

    def tall(mask):
        return jnp.repeat(mask.astype(jnp.float32), tile)[:, None]

    def wide(mask):
        return jnp.repeat(mask.astype(jnp.float32), tile)[None, :]

    cols = jnp.concatenate([strips[k] for k in range(panels)], axis=1)
    lowers, uppers = [], []
    for k in range(panels):
        gone = jnp.any(global_rows[:, None] == pivots[None, : k + 1], axis=1)
        opened = jnp.logical_not((local_cols == 0) & (holder <= k))
        lower = mm(cols[:, :tile], upper_inv[k]) * tall(pattern[:, k] != 0)
        upper = mm(lower_inv[k], rows[:tile])
        lowers.append(lower)
        uppers.append(upper)
        if k + 1 < panels:
            low_x = mm(cross[tile:, :tile], upper_inv[k]) * tall(pivot_pattern[k + 1 :, k] != 0)
            up_x = mm(lower_inv[k], cross[:tile, tile:])
            ok = jnp.repeat(jnp.repeat(cross_flag[k + 1 :, k + 1 :], tile, 0), tile, 1)
            cross = cross[tile:, tile:] - jnp.where(ok != 0, mm(low_x, up_x), 0.0)
            col_ok = (col_flag[:, k + 1 :] != 0) & jnp.logical_not(gone)[:, None]
            col_ok = jnp.repeat(jnp.repeat(col_ok, tile, 0), tile, 1)
            col_new = cols[:, tile:] - jnp.where(col_ok, mm(lower, up_x), 0.0)
            here = tall(global_rows == pivots[k]) != 0
            cols = jnp.where(here, jnp.tile(up_x, (rows_loc, 1)), col_new)
            row_ok = (row_flag[k + 1 :] != 0) & opened[None, :]
            row_ok = jnp.repeat(jnp.repeat(row_ok, tile, 0), tile, 1)
            row_new = rows[tile:] - jnp.where(row_ok, mm(low_x, upper), 0.0)
            first = jnp.where(holder == k, low_x, row_new[:, :tile])
            rows = lax.dynamic_update_slice(row_new, first, (0, 0))
    gone = [jnp.any(global_rows[:, None] == pivots[None, : k + 1], axis=1) for k in range(panels)]
    opened = [jnp.logical_not((local_cols == 0) & (holder <= k)) for k in range(panels)]
    left = jnp.concatenate(
        [jnp.where(tall(gone[k]) != 0, 0.0, lowers[k]) for k in range(panels)], axis=1
    )
    right = jnp.concatenate(
        [jnp.where(wide(opened[k]) != 0, uppers[k], 0.0) for k in range(panels)], axis=0
    )
    alive = jnp.repeat(jnp.repeat(live_local != 0, tile, 0), tile, 1)
    out = matrix - jnp.where(alive, mm(left, right), 0.0)
    first = out[:, :tile]
    for k in range(panels):
        first = jnp.where((holder == k) & (tall(gone[k]) == 0), lowers[k], first)
    out = lax.dynamic_update_slice(out, first, (0, 0))
    for k in range(panels):
        at = (owner_loc[k] * tile, jnp.int32(0))
        old = lax.dynamic_slice(out, at, (tile, width))
        new = jnp.where((row_dev == owner[k]) & (wide(opened[k]) != 0), uppers[k], old)
        out = lax.dynamic_update_slice(out, new, at)
    return out


def solution(mesh):
    in_specs = (P("row", "col"), P("row", None), P("row", "col", None, None), P(), P(), P())
    return jax.shard_map(
        functools.partial(body, mesh),
        mesh=mesh,
        in_specs=in_specs,
        out_specs=P("row", "col"),
        check_vma=False,
    )
```
